32 devices in a mesh: emb: 4 (over y, core), seq: 8 (over z, x).
Axes of the slice: x: 2, y: 2, z: 4, core: 2. Of those that a mesh axis runs over, the one named last changes fastest.
Arguments:
- item_ids: int32 [32, 512], P(None, 'seq'), may hold values from 0 to 16383
- action_ids: int32 [32, 512], P(None, 'seq'), may hold values from 0 to 127
- hist_len: int32 [128], replicated, may hold values from 1 to 509, as said below
- hist_owner: int32 [128], replicated, may hold values from 0 to 31, as said below
- item_table: bfloat16 [16384, 1024], P(None, 'emb'), may hold values from -150 to 150
- action_table: bfloat16 [128, 1024], P(None, 'emb'), may hold values from -6 to 6
- w_in: bfloat16 [1024, 4096], replicated, may hold values from -0.1875 to 0.1875
- w_out: bfloat16 [1024, 1024], replicated, may hold values from -0.1875 to 0.1875
- cotangent: bfloat16 [16384, 1024], P(('emb', 'seq')), may hold values from -6 to 6
Outputs:
- history_out: bfloat16 [16384, 1024], P(('emb', 'seq'))
- row_grads: bfloat16 [32, 512, 1024], P(None, 'seq', 'emb')
- w_in_grad: float32 [1024, 4096], P(('emb', 'seq'))
- w_out_grad: float32 [1024, 1024], P(('emb', 'seq'))
The draws below stay inside these ranges and needn't reach their ends.
Inputs may be any that keep to these rules, and one draw needn't show every extreme that they name: `hist_len`: every owner has exactly 4 histories, whose lengths sum to at most 512; in every draw some owner's lengths sum to exactly 512. Ids at slots past an owner's histories are ignored. `hist_owner`: each owner number appears exactly 4 times.
All inputs are finite; a program needn't handle non-finite values.
Results may differ from the reference program's by a relative error of at most 0.015.
Values may be sent and summed in bfloat16 or wider, within the bound.
A program may use at most 128 MiB of HBM per device.

```python
import math
import jax
import jax.numpy as jnp
import numpy as np
from jax import lax

D = 1024
HEADS = 4
HEAD = 256
ITEMS = 16384
ACTIONS = 128
CAP = 512
HPO = 4
OWNERS = 32


def history_plan(key):
    base = jax.random.fold_in(key, 11)
    pair_count = OWNERS // 2
    spare = jax.random.randint(jax.random.fold_in(base, 1), (pair_count,), 0, CAP - HPO + 1)
    forced = jax.random.randint(jax.random.fold_in(base, 2), (), 0, pair_count)
    spare = jnp.where(jnp.arange(pair_count, dtype=jnp.int32) == forced, 0, spare).astype(jnp.int32)
    totals = jnp.stack([CAP - spare, HPO + spare], axis=1).reshape(OWNERS).astype(jnp.int32)
    totals = jax.random.permutation(jax.random.fold_in(base, 3), totals)
    room = totals - HPO
    raw_cuts = jax.random.randint(jax.random.fold_in(base, 4), (OWNERS, HPO - 1), 0, CAP)
    cuts = jnp.sort(raw_cuts % (room[:, None] + 1), axis=1)
    cuts = jnp.where((totals == CAP)[:, None], room[:, None], cuts)
    edges = jnp.concatenate([jnp.zeros((OWNERS, 1), jnp.int32), cuts.astype(jnp.int32), room[:, None]], axis=1)
    parts = (edges[:, 1:] - edges[:, :-1] + 1).reshape(OWNERS * HPO).astype(jnp.int32)
    order = jax.random.permutation(jax.random.fold_in(base, 5), OWNERS * HPO)
    lengths = jnp.zeros((OWNERS * HPO,), jnp.int32).at[order].set(parts)
    owner_list = jnp.repeat(jnp.arange(OWNERS, dtype=jnp.int32), HPO)
    owner_of = jnp.zeros((OWNERS * HPO,), jnp.int32).at[order].set(owner_list)
    return (lengths, owner_of)


def draw_hist_len(key, part):
    return history_plan(key)[0]


def draw_hist_owner(key, part):
    return history_plan(key)[1]


def draw_item_table(key, part):
    base = jax.random.fold_in(key, 21)
    entries = jnp.clip(jax.random.normal(jax.random.fold_in(base, 1), (ITEMS, D), jnp.float32), -5.0, 5.0)
    return entries.astype(jnp.bfloat16)


def plant(values, key, low, high):
    place = [jax.random.randint(jax.random.fold_in(key, axis), (), 0, length) for axis, length in enumerate(values.shape)]
    main_axis = values.shape.index(max(values.shape))
    beside = place[:main_axis] + [(place[main_axis] + 1) % values.shape[main_axis]] + place[main_axis + 1:]
    return values.at[tuple(place)].set(low).at[tuple(beside)].set(high)


def block_levels(key, shape, cuts, smallest, top_value):
    loudness = 1.0
    for axis_at, shards_of in cuts:
        heights = jax.random.uniform(jax.random.fold_in(jax.random.fold_in(key, 6), axis_at), (shards_of,), jnp.float32, smallest / len(cuts), top_value / len(cuts))
        loudness = loudness * jnp.repeat(jnp.exp(heights), shape[axis_at] // shards_of).reshape((-1,) + (1,) * (len(shape) - 1 - axis_at))
    return loudness


def rank_bounds(number_of, skew):
    loads = [(1 << 20) // math.isqrt(grade ** skew) + 1 for grade in range(1, number_of + 1)]
    scale = 1 + sum(loads) // (1 << 30)
    return np.cumsum(np.array([max(1, weight // scale) for weight in loads]))


def ranked_ids(own_key, shape, number_of, skew):
    grid = rank_bounds(number_of, skew)
    ticket = jax.random.randint(jax.random.fold_in(own_key, 1), shape, 0, int(grid[number_of - 1]))
    standing = jnp.searchsorted(jnp.asarray(grid, jnp.int32), ticket, side="right")
    return jax.random.permutation(jax.random.fold_in(own_key, 2), number_of)[standing].astype(jnp.int32)


def bell_draw(stream_key, shape, width, most, shards=(), kind=jnp.bfloat16):
    drawn = width * jax.random.normal(stream_key, shape, jnp.float32)
    if shards:
        drawn = drawn * block_levels(stream_key, shape, shards, -0.22, 0.18)
    return jnp.clip(drawn, -most, most).astype(kind)


def setup_inputs(seed: int = 0) -> dict:
    splits = jax.random.split(jax.random.key(seed), 10)
    return {
        "item_ids": plant(ranked_ids(splits[0], (OWNERS, CAP), ITEMS, 2), jax.random.fold_in(splits[0], 3), 0, ITEMS - 1).astype(jnp.int32),
        "action_ids": plant(jax.random.randint(splits[1], (OWNERS, CAP), 0, ACTIONS), jax.random.fold_in(splits[1], 1), 0, ACTIONS - 1).astype(jnp.int32),
        "hist_len": draw_hist_len(jax.random.fold_in(splits[9], 71), 0),
        "hist_owner": draw_hist_owner(jax.random.fold_in(splits[9], 71), 0),
        "item_table": draw_item_table(jax.random.fold_in(splits[9], 71), 0),
        "action_table": bell_draw(splits[5], (ACTIONS, D), 1.0, 6.0, ((1, 4),)),
        "w_in": bell_draw(splits[6], (D, 4 * D), D ** -0.5, 0.1875),
        "w_out": bell_draw(splits[7], (D, D), D ** -0.5, 0.1875),
        "cotangent": bell_draw(splits[8], (OWNERS * CAP, D), 1.0, 6.0, ((0, 32),)),
    }


EPSILON = 1e-06

def layer_norm(values):
    centred = values - lax.optimization_barrier(jnp.mean(values, axis=-1, keepdims=True))
    spread = lax.optimization_barrier(jnp.mean(centred * centred, axis=-1, keepdims=True))
    return centred * lax.rsqrt(spread + EPSILON)

def slot_layout(hist_len, hist_owner, owner_index, slot_count):
    chosen = hist_owner == owner_index
    lengths = jnp.where(chosen, hist_len, 0).astype(jnp.int32)
    hist_ends = jnp.cumsum(lengths, dtype=jnp.int32)
    starts = (hist_ends - lengths).astype(jnp.int32)
    slot_index = jnp.arange(slot_count, dtype=jnp.int32)
    inside = chosen[None, :] & (starts[None, :] <= slot_index[:, None]) & (slot_index[:, None] < hist_ends[None, :])
    slot_start = lax.optimization_barrier(jnp.sum(jnp.where(inside, starts[None, :], 0), axis=1, dtype=jnp.int32))
    occupied = jnp.any(inside, axis=1)
    return (slot_start, occupied)

def mixer(pre_values, slot_start, occupied):
    row_count = pre_values.shape[0]
    activated = jax.nn.silu(pre_values).astype(jnp.bfloat16)
    gate_part, value_part, query_part, key_part = jnp.split(activated, 4, axis=1)
    queries = query_part.reshape(row_count, HEADS, HEAD).astype(jnp.float32)
    key_heads = key_part.reshape(row_count, HEADS, HEAD).astype(jnp.float32)
    scores = jnp.einsum('ihd,jhd->hij', queries, key_heads)
    positions = jnp.arange(row_count, dtype=jnp.int32)
    allowed = (positions[None, :] <= positions[:, None]) & (positions[None, :] >= slot_start[:, None]) & occupied[:, None]
    weights = jnp.where(allowed[None], jax.nn.silu(scores * HEAD ** (-0.5)) / CAP, 0.0).astype(jnp.bfloat16)
    value_heads = value_part.reshape(row_count, HEADS, HEAD).astype(jnp.float32)
    mixed_heads = jnp.einsum('hij,jhd->ihd', weights.astype(jnp.float32), value_heads).reshape(row_count, D)
    return layer_norm(mixed_heads) * gate_part.astype(jnp.float32)

def owner_pass(x_rows, grad_rows, slot_start, occupied, w_in, w_out):
    normed = layer_norm(x_rows.astype(jnp.float32)).astype(jnp.bfloat16)
    pre_act = jnp.dot(normed, w_in, preferred_element_type=jnp.float32)
    gated_f32, mixer_back = jax.vjp(lambda pre_values: mixer(pre_values, slot_start, occupied), pre_act)
    gated_rows = gated_f32.astype(jnp.bfloat16)
    result = (x_rows.astype(jnp.float32) + jnp.dot(gated_rows, w_out, preferred_element_type=jnp.float32)).astype(jnp.bfloat16)
    gated_grad = jnp.dot(grad_rows, w_out.T, preferred_element_type=jnp.float32).astype(jnp.bfloat16)
    pre_grad = mixer_back(gated_grad.astype(jnp.float32))[0].astype(jnp.bfloat16)
    normed_grad = jnp.dot(pre_grad, w_in.T, preferred_element_type=jnp.float32).astype(jnp.bfloat16)
    unused_value, norm_back = jax.vjp(layer_norm, x_rows.astype(jnp.float32))
    input_grad = (norm_back(normed_grad.astype(jnp.float32))[0] + grad_rows.astype(jnp.float32)) * occupied[:, None]
    in_grad = jnp.dot(normed.T, pre_grad, preferred_element_type=jnp.float32)
    out_grad = jnp.dot(gated_rows.T, grad_rows, preferred_element_type=jnp.float32)
    return (result, input_grad.astype(jnp.bfloat16), in_grad, out_grad)

def reference(item_ids, action_ids, hist_len, hist_owner, item_table, action_table, w_in, w_out, cotangent):
    owner_count = item_ids.shape[0]
    grads_all = cotangent.reshape(owner_count, CAP, D)

    def one_owner(totals, members):
        owner_items, owner_actions, grad_rows, owner_index = members
        slot_start, occupied = slot_layout(hist_len, hist_owner, owner_index, CAP)
        looked = item_table[owner_items].astype(jnp.float32) + action_table[owner_actions].astype(jnp.float32)
        x_rows = looked.astype(jnp.bfloat16) * occupied[:, None]
        result, input_grad, in_grad, out_grad = owner_pass(x_rows, grad_rows, slot_start, occupied, w_in, w_out)
        return ((totals[0] + in_grad, totals[1] + out_grad), (result, input_grad))
    initial = (jnp.zeros((D, 4 * D), jnp.float32), jnp.zeros((D, D), jnp.float32))
    owner_range = jnp.arange(owner_count, dtype=jnp.int32)
    sums, outputs = lax.scan(one_owner, initial, (item_ids, action_ids, grads_all, owner_range))
    results, input_grads = outputs
    return (results.reshape(owner_count * CAP, D), input_grads, sums[0] / owner_count, sums[1] / owner_count)
```

```python
import jax
import jax.numpy as jnp
from jax import lax
from jax.sharding import PartitionSpec as P

D = 1024
HEADS = 4
HEAD = 256
CAP = 512


EPSILON = 1e-06


def layer_norm(values):
    centred = values - jnp.mean(values, axis=-1, keepdims=True)
    spread = jnp.mean(centred * centred, axis=-1, keepdims=True)
    return centred * lax.rsqrt(spread + EPSILON)


def slot_layout(hist_len, hist_owner, owner_index, slot_count):
    chosen = hist_owner == owner_index
    lengths = jnp.where(chosen, hist_len, 0)
    hist_ends = jnp.cumsum(lengths, dtype=jnp.int32)
    starts = hist_ends - lengths
    slot_index = jnp.arange(slot_count, dtype=jnp.int32)
    inside = (
        chosen[None, :]
        & (starts[None, :] <= slot_index[:, None])
        & (slot_index[:, None] < hist_ends[None, :])
    )
    slot_start = jnp.sum(jnp.where(inside, starts[None, :], 0), axis=1, dtype=jnp.int32)
    occupied = jnp.any(inside, axis=1)
    return (slot_start, occupied)


def mixer(pre_values, slot_start, occupied):
    row_count = pre_values.shape[0]
    activated = jax.nn.silu(pre_values).astype(jnp.bfloat16)
    gate_part, value_part, query_part, key_part = jnp.split(activated, 4, axis=1)
    queries = query_part.reshape(row_count, HEADS, HEAD)
    key_heads = key_part.reshape(row_count, HEADS, HEAD)
    scores = jnp.einsum("ihd,jhd->hij", queries, key_heads, preferred_element_type=jnp.float32)
    positions = jnp.arange(row_count, dtype=jnp.int32)
    allowed = (
        (positions[None, :] <= positions[:, None])
        & (positions[None, :] >= slot_start[:, None])
        & occupied[:, None]
    )
    weights = jnp.where(allowed[None], jax.nn.silu(scores * HEAD ** (-0.5)) / CAP, 0.0).astype(
        jnp.bfloat16
    )
    value_heads = value_part.reshape(row_count, HEADS, HEAD)
    mixed_heads = jnp.einsum(
        "hij,jhd->ihd", weights, value_heads, preferred_element_type=jnp.float32
    ).reshape(row_count, D)
    return layer_norm(mixed_heads) * gate_part.astype(jnp.float32)


def local_pass(x_rows, grad_rows, slot_start, occupied, w_in, w_out):
    normed = layer_norm(x_rows.astype(jnp.float32)).astype(jnp.bfloat16)
    pre_act = jnp.dot(normed, w_in, preferred_element_type=jnp.float32)
    gated_f32, mixer_back = jax.vjp(
        lambda pre_values: mixer(pre_values, slot_start, occupied), pre_act
    )
    gated_rows = gated_f32.astype(jnp.bfloat16)
    result = (
        x_rows.astype(jnp.float32) + jnp.dot(gated_rows, w_out, preferred_element_type=jnp.float32)
    ).astype(jnp.bfloat16)
    gated_grad = jnp.dot(grad_rows, w_out.T, preferred_element_type=jnp.float32).astype(
        jnp.bfloat16
    )
    pre_grad = mixer_back(gated_grad.astype(jnp.float32))[0].astype(jnp.bfloat16)
    normed_grad = jnp.dot(pre_grad, w_in.T, preferred_element_type=jnp.float32).astype(jnp.bfloat16)
    unused_value, norm_back = jax.vjp(layer_norm, x_rows.astype(jnp.float32))
    input_grad = (
        norm_back(normed_grad.astype(jnp.float32))[0] + grad_rows.astype(jnp.float32)
    ) * occupied[:, None]
    return (result, input_grad.astype(jnp.bfloat16), normed, pre_grad, gated_rows)


def axis_bits(name):
    return [(name, bit) for bit in range(lax.axis_size(name).bit_length() - 1)]


def swap_with(values, bit):
    name, place = bit
    count = lax.axis_size(name)
    return lax.ppermute(values, name, [(at, at ^ (1 << place)) for at in range(count)])


def own_bit(bit):
    return (lax.axis_index(bit[0]) >> bit[1]) & 1


def pick(values, index, axis):
    return lax.dynamic_index_in_dim(values, index, axis, keepdims=False)


def column_groups(total, groups):
    unit = total // groups // 128 * 128
    edges = [unit * at for at in range(groups)] + [total]
    return list(zip(edges[:-1], edges[1:]))


def reduce_rows(left, right, groups):
    emb_bits, seq_bits = axis_bits("emb"), axis_bits("seq")
    names = emb_bits[::-1] + seq_bits[::-1]
    rows = left.shape[1]
    block = rows >> len(names)
    first = names[len(emb_bits) - 1]
    others = emb_bits[1:2] + seq_bits[:2]
    tail = emb_bits[2:] + seq_bits[2:]
    at = names.index(first)
    split = left.reshape(left.shape[0], 1 << at, 2, rows >> (at + 1))
    mine_bit = own_bit(first)

    def product(which, low, high):
        chosen = pick(split, which, 2).reshape(left.shape[0], rows // 2)
        return jnp.dot(chosen.T, right[:, low:high], preferred_element_type=jnp.float32)

    spans = column_groups(right.shape[1], groups)
    live = []
    arrived = [swap_with(product(1 - mine_bit, *span).astype(jnp.bfloat16), first) for span in spans]
    for span, part in zip(spans, arrived):
        total = (product(mine_bit, *span) + part.astype(jnp.float32)).astype(jnp.bfloat16)
        live.append(total)
    left_names = [name for name in names if name != first]
    state = []
    for at_group, total in enumerate(live):
        turn = at_group % len(others)
        order = others[turn:] + others[:turn] + tail
        state.append([total, list(left_names), order])
    for step in range(len(left_names)):
        for entry in state:
            total, held, order = entry
            bit = order[step]
            place = held.index(bit)
            width = total.shape[-1]
            shaped = total.reshape(1 << place, 2, total.shape[0] >> (place + 1), width)
            mine_bit = own_bit(bit)
            sent = pick(shaped, 1 - mine_bit, 1)
            kept = pick(shaped, mine_bit, 1)
            summed = kept.astype(jnp.float32) + swap_with(sent, bit).astype(jnp.float32)
            if step + 1 < len(left_names):
                summed = summed.astype(jnp.bfloat16)
            entry[0] = summed.reshape(total.shape[0] // 2, width)
            held.remove(bit)
    return jnp.concatenate([entry[0] for entry in state], axis=1)


def shards(
    item_ids, action_ids, hist_len, hist_owner, item_table, action_table, w_in, w_out, cotangent
):
    emb_count = lax.axis_size("emb")
    seq_count = lax.axis_size("seq")
    device_count = emb_count * seq_count
    owner_count = item_ids.shape[0]
    slot_rows = item_ids.shape[1]
    column_width = item_table.shape[1]
    looked_items = jnp.take(item_table, item_ids, axis=0).astype(jnp.float32)
    action_hot = (
        action_ids[:, :, None] == jnp.arange(action_table.shape[0], dtype=jnp.int32)
    ).astype(jnp.bfloat16)
    looked_actions = jnp.einsum(
        "osa,ac->osc", action_hot, action_table, preferred_element_type=jnp.float32
    )
    looked = (looked_items + looked_actions).astype(jnp.bfloat16)
    arrived = lax.all_to_all(looked, ("emb", "seq"), split_axis=0, concat_axis=0, tiled=True)
    x_rows = (
        arrived.reshape(emb_count, seq_count, slot_rows, column_width)
        .transpose(1, 2, 0, 3)
        .reshape(seq_count * slot_rows, emb_count * column_width)
    )
    owner_index = lax.axis_index(("emb", "seq"))
    slot_start, occupied = slot_layout(hist_len, hist_owner, owner_index, x_rows.shape[0])
    x_rows = x_rows * occupied[:, None]
    result, input_grad, normed, pre_grad, gated_rows = local_pass(
        x_rows, cotangent, slot_start, occupied, w_in, w_out
    )
    outgoing = (
        input_grad.reshape(seq_count, slot_rows, emb_count, column_width)
        .transpose(2, 0, 1, 3)
        .reshape(owner_count, slot_rows, column_width)
    )
    row_grads = lax.all_to_all(outgoing, ("emb", "seq"), split_axis=0, concat_axis=0, tiled=True)
    out_share = reduce_rows(gated_rows, cotangent, 1)
    in_share = reduce_rows(normed, pre_grad, 3)
    return (result, row_grads, in_share / device_count, out_share / device_count)


def solution(mesh):
    in_specs = (
        P(None, "seq"),
        P(None, "seq"),
        P(),
        P(),
        P(None, "emb"),
        P(None, "emb"),
        P(),
        P(),
        P(("emb", "seq"), None),
    )
    out_specs = (
        P(("emb", "seq"), None),
        P(None, "seq", "emb"),
        P(("emb", "seq"), None),
        P(("emb", "seq"), None),
    )
    return jax.shard_map(shards, mesh=mesh, in_specs=in_specs, out_specs=out_specs, check_vma=False)
```

```python
import jax
import jax.numpy as jnp
from jax import lax
from jax.experimental import pallas as pl
from jax.experimental.pallas import tpu as pltpu
from jax.sharding import PartitionSpec as P

D = 1024
HEADS = 4
HEAD = 256
CAP = 512
TILE = 256
STRIP = 16
NT = (((1,), (1,)), ((), ()))
TN = (((0,), (0,)), ((), ()))


EPSILON = 1e-06


def layer_norm(values):
    centred = values - jnp.mean(values, axis=-1, keepdims=True)
    spread = jnp.mean(centred * centred, axis=-1, keepdims=True)
    return centred * lax.rsqrt(spread + EPSILON)


def slot_layout(hist_len, hist_owner, owner_index, slot_count):
    chosen = hist_owner == owner_index
    lengths = jnp.where(chosen, hist_len, 0)
    hist_ends = jnp.cumsum(lengths, dtype=jnp.int32)
    starts = hist_ends - lengths
    slot_index = jnp.arange(slot_count, dtype=jnp.int32)
    inside = (
        chosen[None, :]
        & (starts[None, :] <= slot_index[:, None])
        & (slot_index[:, None] < hist_ends[None, :])
    )
    slot_start = jnp.sum(jnp.where(inside, starts[None, :], 0), axis=1, dtype=jnp.int32)
    occupied = jnp.any(inside, axis=1)
    return (slot_start, occupied)


def head_weights(queries, keys, lower_ref, row_at, limit):
    tile = queries.shape[0]
    scaled = (
        lax.dot_general(queries, keys, NT, preferred_element_type=jnp.float32) * HEAD ** (-0.5)
    )
    rows = row_at + lax.broadcasted_iota(jnp.int32, (tile, limit), 0)
    columns = lax.broadcasted_iota(jnp.int32, (tile, limit), 1)
    allowed = (columns <= rows) & (columns >= lower_ref[pl.ds(row_at, tile), :])
    return scaled, jax.nn.sigmoid(scaled), allowed


def mixing_kernel(lower_ref, gate_ref, value_ref, query_ref, key_ref, mixed_ref, gated_ref, held):
    head = pl.program_id(0)
    row_count = value_ref.shape[0]
    held[0] = jax.nn.silu(value_ref[...]).astype(jnp.bfloat16)
    held[1] = jax.nn.silu(query_ref[...]).astype(jnp.bfloat16)
    held[2] = jax.nn.silu(key_ref[...]).astype(jnp.bfloat16)
    columns = pl.ds(pl.multiple_of(head * HEAD, HEAD), HEAD)
    for row_at in range(0, row_count, TILE):
        limit = row_at + TILE
        scaled, sigmoid, allowed = head_weights(
            held[1, row_at:limit, :], held[2, :limit, :], lower_ref, row_at, limit
        )
        weights = jnp.where(allowed, scaled * sigmoid / CAP, 0.0).astype(jnp.bfloat16)
        mixed_ref[row_at:limit, columns] = jnp.dot(
            weights, held[0, :limit, :], preferred_element_type=jnp.float32
        )

    @pl.when(head == HEADS - 1)
    def finish():
        def rows_step(at, carry):
            rows = pl.ds(pl.multiple_of(at * STRIP, STRIP), STRIP)
            gate = jax.nn.silu(gate_ref[rows, :]).astype(jnp.bfloat16).astype(jnp.float32)
            gated_ref[rows, :] = (layer_norm(mixed_ref[rows, :]) * gate).astype(jnp.bfloat16)
            return carry

        lax.fori_loop(0, row_count // STRIP, rows_step, 0)


def silu_back(pre_values, grads):
    sigmoid = jax.nn.sigmoid(pre_values)
    rounded = grads.astype(jnp.bfloat16).astype(jnp.float32)
    return (rounded * (sigmoid * (1.0 + pre_values * (1.0 - sigmoid)))).astype(jnp.bfloat16)


def mixing_back_kernel(
    lower_ref,
    gate_ref,
    value_ref,
    query_ref,
    key_ref,
    mixed_ref,
    grad_ref,
    out_ref,
    mixed_grad,
    held,
    value_sum,
    key_sum,
):
    head = pl.program_id(0)
    row_count = value_ref.shape[0]

    @pl.when(head == 0)
    def begin():
        def rows_step(at, carry):
            rows = pl.ds(pl.multiple_of(at * STRIP, STRIP), STRIP)
            pre_gate = gate_ref[rows, :]
            gate = jax.nn.silu(pre_gate).astype(jnp.bfloat16).astype(jnp.float32)
            grads = grad_ref[rows, :].astype(jnp.float32)
            values = mixed_ref[rows, :]
            centred = values - jnp.mean(values, axis=-1, keepdims=True)
            inverse = lax.rsqrt(jnp.mean(centred * centred, axis=-1, keepdims=True) + EPSILON)
            normal = centred * inverse
            out_ref[rows, :D] = silu_back(pre_gate, grads * normal)
            back = grads * gate
            along = jnp.mean(back * normal, axis=-1, keepdims=True)
            level = jnp.mean(back, axis=-1, keepdims=True)
            mixed_grad[rows, :] = (inverse * (back - level - normal * along)).astype(jnp.bfloat16)
            return carry

        lax.fori_loop(0, row_count // STRIP, rows_step, 0)

    held[0] = jax.nn.silu(value_ref[...]).astype(jnp.bfloat16)
    held[1] = jax.nn.silu(query_ref[...]).astype(jnp.bfloat16)
    held[2] = jax.nn.silu(key_ref[...]).astype(jnp.bfloat16)
    columns = pl.ds(pl.multiple_of(head * HEAD, HEAD), HEAD)
    value_sum[...] = jnp.zeros_like(value_sum)
    key_sum[...] = jnp.zeros_like(key_sum)
    for row_at in range(0, row_count, TILE):
        limit = row_at + TILE
        queries, keys = held[1, row_at:limit, :], held[2, :limit, :]
        scaled, sigmoid, allowed = head_weights(queries, keys, lower_ref, row_at, limit)
        weights = jnp.where(allowed, scaled * sigmoid / CAP, 0.0).astype(jnp.bfloat16)
        rows_grad = mixed_grad[row_at:limit, columns]
        value_sum[:limit, :] += lax.dot_general(
            weights, rows_grad, TN, preferred_element_type=jnp.float32
        )
        weight_grad = lax.dot_general(
            rows_grad, held[0, :limit, :], NT, preferred_element_type=jnp.float32
        ).astype(jnp.bfloat16).astype(jnp.float32)
        score_grad = jnp.where(
            allowed,
            weight_grad * (sigmoid * (1.0 + scaled * (1.0 - sigmoid))) * (HEAD ** (-0.5) / CAP),
            0.0,
        ).astype(jnp.bfloat16)
        query_grad = jnp.dot(score_grad, keys, preferred_element_type=jnp.float32)
        place = pl.ds(pl.multiple_of(2 * D + head * HEAD, HEAD), HEAD)
        out_ref[row_at:limit, place] = silu_back(query_ref[row_at:limit, :], query_grad)
        key_sum[:limit, :] += lax.dot_general(
            score_grad, queries, TN, preferred_element_type=jnp.float32
        )
    place = pl.ds(pl.multiple_of(D + head * HEAD, HEAD), HEAD)
    out_ref[:, place] = silu_back(value_ref[...], value_sum[...])
    place = pl.ds(pl.multiple_of(3 * D + head * HEAD, HEAD), HEAD)
    out_ref[:, place] = silu_back(key_ref[...], key_sum[...])


def part_specs(rows):
    return [
        pl.BlockSpec((rows, 1), lambda head: (0, 0)),
        pl.BlockSpec((rows, D), lambda head: (0, 0)),
        pl.BlockSpec((rows, HEAD), lambda head: (0, HEADS + head)),
        pl.BlockSpec((rows, HEAD), lambda head: (0, 2 * HEADS + head)),
        pl.BlockSpec((rows, HEAD), lambda head: (0, 3 * HEADS + head)),
    ]


def mix(lower, pre_act):
    rows = pre_act.shape[0]
    whole = pl.BlockSpec((rows, D), lambda head: (0, 0))
    return pl.pallas_call(
        mixing_kernel,
        grid=(HEADS,),
        in_specs=part_specs(rows),
        out_specs=[whole, whole],
        out_shape=[
            jax.ShapeDtypeStruct((rows, D), jnp.float32),
            jax.ShapeDtypeStruct((rows, D), jnp.bfloat16),
        ],
        scratch_shapes=[pltpu.VMEM((3, rows, HEAD), jnp.bfloat16)],
        compiler_params=pltpu.CompilerParams(vmem_limit_bytes=40 * 2**20),
        cost_estimate=pl.CostEstimate(flops=10**10, bytes_accessed=14 * 2**20, transcendentals=0),
    )(lower, pre_act, pre_act, pre_act, pre_act)


def mix_back(lower, pre_act, mixed, gated_grad):
    rows = pre_act.shape[0]
    whole = pl.BlockSpec((rows, D), lambda head: (0, 0))
    return pl.pallas_call(
        mixing_back_kernel,
        grid=(HEADS,),
        in_specs=part_specs(rows) + [whole, whole],
        out_specs=pl.BlockSpec((rows, 4 * D), lambda head: (0, 0)),
        out_shape=jax.ShapeDtypeStruct((rows, 4 * D), jnp.bfloat16),
        scratch_shapes=[
            pltpu.VMEM((rows, D), jnp.bfloat16),
            pltpu.VMEM((3, rows, HEAD), jnp.bfloat16),
            pltpu.VMEM((rows, HEAD), jnp.float32),
            pltpu.VMEM((rows, HEAD), jnp.float32),
        ],
        compiler_params=pltpu.CompilerParams(vmem_limit_bytes=48 * 2**20),
        cost_estimate=pl.CostEstimate(
            flops=2 * 10**10, bytes_accessed=18 * 2**20, transcendentals=0
        ),
    )(lower, pre_act, pre_act, pre_act, pre_act, mixed, gated_grad)


def local_pass(x_rows, grad_rows, slot_start, occupied, w_in, w_out, gated_grad):
    row_count = x_rows.shape[0]
    normed = layer_norm(x_rows.astype(jnp.float32)).astype(jnp.bfloat16)
    pre_act = jnp.dot(normed, w_in, preferred_element_type=jnp.float32)
    lower = jnp.where(occupied, slot_start, row_count)[:, None]
    mixed, gated_rows = mix(lower, pre_act)
    out_share = reduce_rows(gated_rows, grad_rows, 1)
    result = (
        x_rows.astype(jnp.float32) + jnp.dot(gated_rows, w_out, preferred_element_type=jnp.float32)
    ).astype(jnp.bfloat16)
    pre_grad = mix_back(lower, pre_act, mixed, gated_grad)
    normed_grad = jnp.dot(pre_grad, w_in.T, preferred_element_type=jnp.float32).astype(jnp.bfloat16)
    unused_value, norm_back = jax.vjp(layer_norm, x_rows.astype(jnp.float32))
    input_grad = (
        norm_back(normed_grad.astype(jnp.float32))[0] + grad_rows.astype(jnp.float32)
    ) * occupied[:, None]
    return (result, input_grad.astype(jnp.bfloat16), normed, pre_grad, out_share)


def axis_bits(name):
    return [(name, bit) for bit in range(lax.axis_size(name).bit_length() - 1)]


def swap_with(values, bit):
    name, place = bit
    count = lax.axis_size(name)
    return lax.ppermute(values, name, [(at, at ^ (1 << place)) for at in range(count)])


def own_bit(bit):
    return (lax.axis_index(bit[0]) >> bit[1]) & 1


def pick(values, index, axis):
    return lax.dynamic_index_in_dim(values, index, axis, keepdims=False)


def column_groups(total, groups):
    unit = total // groups // 128 * 128
    edges = [unit * at for at in range(groups)] + [total]
    return list(zip(edges[:-1], edges[1:]))


def reduce_rows(left, right, groups):
    emb_bits, seq_bits = axis_bits("emb"), axis_bits("seq")
    names = emb_bits[::-1] + seq_bits[::-1]
    rows = left.shape[1]
    block = rows >> len(names)
    first = names[len(emb_bits) - 1]
    others = emb_bits[1:2] + seq_bits[:2]
    tail = emb_bits[2:] + seq_bits[2:]
    at = names.index(first)
    piece = rows >> (at + 1)
    mine_bit = own_bit(first)

    def half(which):
        cuts = [
            lax.dynamic_slice_in_dim(left, (2 * part + which) * piece, piece, 1)
            for part in range(1 << at)
        ]
        return jnp.concatenate(cuts, axis=1)

    halves = {"kept": half(mine_bit), "sent": half(1 - mine_bit)}

    def product(which, low, high):
        return jnp.dot(
            halves[which].T, right[:, low:high], preferred_element_type=jnp.float32
        )

    spans = column_groups(right.shape[1], groups)
    live = []
    arrived = [swap_with(product("sent", *span).astype(jnp.bfloat16), first) for span in spans]
    for span, part in zip(spans, arrived):
        total = (product("kept", *span) + part.astype(jnp.float32)).astype(jnp.bfloat16)
        live.append(total)
    left_names = [name for name in names if name != first]
    state = []
    for at_group, total in enumerate(live):
        turn = at_group % len(others)
        order = others[turn:] + others[:turn] + tail
        state.append([total, list(left_names), order])
    for step in range(len(left_names)):
        for entry in state:
            total, held, order = entry
            bit = order[step]
            place = held.index(bit)
            width = total.shape[-1]
            shaped = total.reshape(1 << place, 2, total.shape[0] >> (place + 1), width)
            mine_bit = own_bit(bit)
            sent = pick(shaped, 1 - mine_bit, 1)
            kept = pick(shaped, mine_bit, 1)
            summed = kept.astype(jnp.float32) + swap_with(sent, bit).astype(jnp.float32)
            if step + 1 < len(left_names):
                summed = summed.astype(jnp.bfloat16)
            entry[0] = summed.reshape(total.shape[0] // 2, width)
            held.remove(bit)
    return jnp.concatenate([entry[0] for entry in state], axis=1)


def shards(
    item_ids, action_ids, hist_len, hist_owner, item_table, action_table, w_in, w_out, cotangent
):
    emb_count = lax.axis_size("emb")
    seq_count = lax.axis_size("seq")
    device_count = emb_count * seq_count
    owner_count = item_ids.shape[0]
    slot_rows = item_ids.shape[1]
    column_width = item_table.shape[1]
    looked_items = jnp.take(item_table, item_ids, axis=0).astype(jnp.float32)
    action_hot = (
        action_ids[:, :, None] == jnp.arange(action_table.shape[0], dtype=jnp.int32)
    ).astype(jnp.bfloat16)
    looked_actions = jnp.einsum(
        "osa,ac->osc", action_hot, action_table, preferred_element_type=jnp.float32
    )
    looked = (looked_items + looked_actions).astype(jnp.bfloat16)
    arrived = lax.all_to_all(looked, ("emb", "seq"), split_axis=0, concat_axis=0, tiled=True)
    x_rows = (
        arrived.reshape(emb_count, seq_count, slot_rows, column_width)
        .transpose(1, 2, 0, 3)
        .reshape(seq_count * slot_rows, emb_count * column_width)
    )
    owner_index = lax.axis_index(("emb", "seq"))
    slot_start, occupied = slot_layout(hist_len, hist_owner, owner_index, x_rows.shape[0])
    x_rows = x_rows * occupied[:, None]
    gated_grad = jnp.dot(cotangent, w_out.T, preferred_element_type=jnp.float32).astype(
        jnp.bfloat16
    )
    result, input_grad, normed, pre_grad, out_share = local_pass(
        x_rows, cotangent, slot_start, occupied, w_in, w_out, gated_grad
    )
    outgoing = (
        input_grad.reshape(seq_count, slot_rows, emb_count, column_width)
        .transpose(2, 0, 1, 3)
        .reshape(owner_count, slot_rows, column_width)
    )
    row_grads = lax.all_to_all(outgoing, ("emb", "seq"), split_axis=0, concat_axis=0, tiled=True)
    in_share = reduce_rows(normed, pre_grad, 3)
    return (result, row_grads, in_share / device_count, out_share / device_count)


def solution(mesh):
    in_specs = (
        P(None, "seq"),
        P(None, "seq"),
        P(),
        P(),
        P(None, "emb"),
        P(None, "emb"),
        P(),
        P(),
        P(("emb", "seq"), None),
    )
    out_specs = (
        P(("emb", "seq"), None),
        P(None, "seq", "emb"),
        P(("emb", "seq"), None),
        P(("emb", "seq"), None),
    )
    return jax.shard_map(shards, mesh=mesh, in_specs=in_specs, out_specs=out_specs, check_vma=False)
```

```python
import jax
import jax.numpy as jnp
from jax import lax
from jax.experimental import pallas as pl
from jax.experimental.pallas import tpu as pltpu
from jax.sharding import PartitionSpec as P

D = 1024
HEADS = 4
HEAD = 256
CAP = 512
TILE = 256
STRIP = 16
NT = (((1,), (1,)), ((), ()))
TN = (((0,), (0,)), ((), ()))


EPSILON = 1e-06


def layer_norm(values):
    centred = values - jnp.mean(values, axis=-1, keepdims=True)
    spread = jnp.mean(centred * centred, axis=-1, keepdims=True)
    return centred * lax.rsqrt(spread + EPSILON)


def slot_layout(hist_len, hist_owner, owner_index, slot_count):
    chosen = hist_owner == owner_index
    lengths = jnp.where(chosen, hist_len, 0)
    hist_ends = jnp.cumsum(lengths, dtype=jnp.int32)
    starts = hist_ends - lengths
    slot_index = jnp.arange(slot_count, dtype=jnp.int32)
    inside = (
        chosen[None, :]
        & (starts[None, :] <= slot_index[:, None])
        & (slot_index[:, None] < hist_ends[None, :])
    )
    slot_start = jnp.sum(jnp.where(inside, starts[None, :], 0), axis=1, dtype=jnp.int32)
    occupied = jnp.any(inside, axis=1)
    return (slot_start, occupied)


def head_weights(queries, keys, lower_ref, row_at, limit):
    tile = queries.shape[0]
    scaled = (
        lax.dot_general(queries, keys, NT, preferred_element_type=jnp.float32) * HEAD ** (-0.5)
    )
    rows = row_at + lax.broadcasted_iota(jnp.int32, (tile, limit), 0)
    columns = lax.broadcasted_iota(jnp.int32, (tile, limit), 1)
    allowed = (columns <= rows) & (columns >= lower_ref[pl.ds(row_at, tile), :])
    return scaled, jax.nn.sigmoid(scaled), allowed


def mixing_kernel(lower_ref, gate_ref, value_ref, query_ref, key_ref, mixed_ref, gated_ref, held):
    head = pl.program_id(0)
    row_count = value_ref.shape[0]
    held[0] = jax.nn.silu(value_ref[...]).astype(jnp.bfloat16)
    held[1] = jax.nn.silu(query_ref[...]).astype(jnp.bfloat16)
    held[2] = jax.nn.silu(key_ref[...]).astype(jnp.bfloat16)
    columns = pl.ds(pl.multiple_of(head * HEAD, HEAD), HEAD)
    for row_at in range(0, row_count, TILE):
        limit = row_at + TILE
        scaled, sigmoid, allowed = head_weights(
            held[1, row_at:limit, :], held[2, :limit, :], lower_ref, row_at, limit
        )
        weights = jnp.where(allowed, scaled * sigmoid / CAP, 0.0).astype(jnp.bfloat16)
        mixed_ref[row_at:limit, columns] = jnp.dot(
            weights, held[0, :limit, :], preferred_element_type=jnp.float32
        )

    @pl.when(head == HEADS - 1)
    def finish():
        def rows_step(at, carry):
            rows = pl.ds(pl.multiple_of(at * STRIP, STRIP), STRIP)
            gate = jax.nn.silu(gate_ref[rows, :]).astype(jnp.bfloat16).astype(jnp.float32)
            gated_ref[rows, :] = (layer_norm(mixed_ref[rows, :]) * gate).astype(jnp.bfloat16)
            return carry

        lax.fori_loop(0, row_count // STRIP, rows_step, 0)


def silu_back(pre_values, grads):
    sigmoid = jax.nn.sigmoid(pre_values)
    rounded = grads.astype(jnp.bfloat16).astype(jnp.float32)
    return (rounded * (sigmoid * (1.0 + pre_values * (1.0 - sigmoid)))).astype(jnp.bfloat16)


def mixing_back_kernel(
    lower_ref,
    gate_ref,
    value_ref,
    query_ref,
    key_ref,
    mixed_ref,
    grad_ref,
    out_ref,
    mixed_grad,
    held,
    value_sum,
    key_sum,
):
    head = pl.program_id(0)
    row_count = value_ref.shape[0]

    @pl.when(head == 0)
    def begin():
        def rows_step(at, carry):
            rows = pl.ds(pl.multiple_of(at * STRIP, STRIP), STRIP)
            pre_gate = gate_ref[rows, :]
            gate = jax.nn.silu(pre_gate).astype(jnp.bfloat16).astype(jnp.float32)
            grads = grad_ref[rows, :].astype(jnp.float32)
            values = mixed_ref[rows, :]
            centred = values - jnp.mean(values, axis=-1, keepdims=True)
            inverse = lax.rsqrt(jnp.mean(centred * centred, axis=-1, keepdims=True) + EPSILON)
            normal = centred * inverse
            out_ref[rows, :D] = silu_back(pre_gate, grads * normal)
            back = grads * gate
            along = jnp.mean(back * normal, axis=-1, keepdims=True)
            level = jnp.mean(back, axis=-1, keepdims=True)
            mixed_grad[rows, :] = (inverse * (back - level - normal * along)).astype(jnp.bfloat16)
            return carry

        lax.fori_loop(0, row_count // STRIP, rows_step, 0)

    held[0] = jax.nn.silu(value_ref[...]).astype(jnp.bfloat16)
    held[1] = jax.nn.silu(query_ref[...]).astype(jnp.bfloat16)
    held[2] = jax.nn.silu(key_ref[...]).astype(jnp.bfloat16)
    columns = pl.ds(pl.multiple_of(head * HEAD, HEAD), HEAD)
    value_sum[...] = jnp.zeros_like(value_sum)
    key_sum[...] = jnp.zeros_like(key_sum)
    for row_at in range(0, row_count, TILE):
        limit = row_at + TILE
        queries, keys = held[1, row_at:limit, :], held[2, :limit, :]
        scaled, sigmoid, allowed = head_weights(queries, keys, lower_ref, row_at, limit)
        weights = jnp.where(allowed, scaled * sigmoid / CAP, 0.0).astype(jnp.bfloat16)
        rows_grad = mixed_grad[row_at:limit, columns]
        value_sum[:limit, :] += lax.dot_general(
            weights, rows_grad, TN, preferred_element_type=jnp.float32
        )
        weight_grad = lax.dot_general(
            rows_grad, held[0, :limit, :], NT, preferred_element_type=jnp.float32
        ).astype(jnp.bfloat16).astype(jnp.float32)
        score_grad = jnp.where(
            allowed,
            weight_grad * (sigmoid * (1.0 + scaled * (1.0 - sigmoid))) * (HEAD ** (-0.5) / CAP),
            0.0,
        ).astype(jnp.bfloat16)
        query_grad = jnp.dot(score_grad, keys, preferred_element_type=jnp.float32)
        place = pl.ds(pl.multiple_of(2 * D + head * HEAD, HEAD), HEAD)
        out_ref[row_at:limit, place] = silu_back(query_ref[row_at:limit, :], query_grad)
        key_sum[:limit, :] += lax.dot_general(
            score_grad, queries, TN, preferred_element_type=jnp.float32
        )
    place = pl.ds(pl.multiple_of(D + head * HEAD, HEAD), HEAD)
    out_ref[:, place] = silu_back(value_ref[...], value_sum[...])
    place = pl.ds(pl.multiple_of(3 * D + head * HEAD, HEAD), HEAD)
    out_ref[:, place] = silu_back(key_ref[...], key_sum[...])


def part_specs(rows):
    return [
        pl.BlockSpec((rows, 1), lambda head: (0, 0)),
        pl.BlockSpec((rows, D), lambda head: (0, 0)),
        pl.BlockSpec((rows, HEAD), lambda head: (0, HEADS + head)),
        pl.BlockSpec((rows, HEAD), lambda head: (0, 2 * HEADS + head)),
        pl.BlockSpec((rows, HEAD), lambda head: (0, 3 * HEADS + head)),
    ]


def mix(lower, pre_act):
    rows = pre_act.shape[0]
    whole = pl.BlockSpec((rows, D), lambda head: (0, 0))
    return pl.pallas_call(
        mixing_kernel,
        grid=(HEADS,),
        in_specs=part_specs(rows),
        out_specs=[whole, whole],
        out_shape=[
            jax.ShapeDtypeStruct((rows, D), jnp.float32),
            jax.ShapeDtypeStruct((rows, D), jnp.bfloat16),
        ],
        scratch_shapes=[pltpu.VMEM((3, rows, HEAD), jnp.bfloat16)],
        compiler_params=pltpu.CompilerParams(vmem_limit_bytes=40 * 2**20),
        cost_estimate=pl.CostEstimate(flops=10**10, bytes_accessed=14 * 2**20, transcendentals=0),
    )(lower, pre_act, pre_act, pre_act, pre_act)


def mix_back(lower, pre_act, mixed, gated_grad):
    rows = pre_act.shape[0]
    whole = pl.BlockSpec((rows, D), lambda head: (0, 0))
    return pl.pallas_call(
        mixing_back_kernel,
        grid=(HEADS,),
        in_specs=part_specs(rows) + [whole, whole],
        out_specs=pl.BlockSpec((rows, 4 * D), lambda head: (0, 0)),
        out_shape=jax.ShapeDtypeStruct((rows, 4 * D), jnp.bfloat16),
        scratch_shapes=[
            pltpu.VMEM((rows, D), jnp.bfloat16),
            pltpu.VMEM((3, rows, HEAD), jnp.bfloat16),
            pltpu.VMEM((rows, HEAD), jnp.float32),
            pltpu.VMEM((rows, HEAD), jnp.float32),
        ],
        compiler_params=pltpu.CompilerParams(vmem_limit_bytes=48 * 2**20),
        cost_estimate=pl.CostEstimate(
            flops=2 * 10**10, bytes_accessed=18 * 2**20, transcendentals=0
        ),
    )(lower, pre_act, pre_act, pre_act, pre_act, mixed, gated_grad)


def local_pass(x_rows, grad_rows, slot_start, occupied, w_in, w_out, gated_grad):
    row_count = x_rows.shape[0]
    normed = layer_norm(x_rows.astype(jnp.float32)).astype(jnp.bfloat16)
    pre_act = jnp.dot(normed, w_in, preferred_element_type=jnp.float32)
    lower = jnp.where(occupied, slot_start, row_count)[:, None]
    mixed, gated_rows = mix(lower, pre_act)
    out_share = reduce_rows(gated_rows, grad_rows, 1)
    result = (
        x_rows.astype(jnp.float32)
        + jnp.dot(gated_rows, w_out, preferred_element_type=jnp.float32)
    ).astype(jnp.bfloat16)
    pre_grad = mix_back(lower, pre_act, mixed, gated_grad)
    normed_grad = jnp.dot(pre_grad, w_in.T, preferred_element_type=jnp.float32).astype(jnp.bfloat16)
    _, norm_back = jax.vjp(layer_norm, x_rows.astype(jnp.float32))
    input_grad = (
        norm_back(normed_grad.astype(jnp.float32))[0] + grad_rows.astype(jnp.float32)
    ) * occupied[:, None]
    return (result, input_grad.astype(jnp.bfloat16), normed, pre_grad, out_share)


def axis_bits(name):
    return [(name, bit) for bit in range(lax.axis_size(name).bit_length() - 1)]


def swap_with(values, bit):
    name, place = bit
    count = lax.axis_size(name)
    return lax.ppermute(values, name, [(at, at ^ (1 << place)) for at in range(count)])


def own_bit(bit):
    return (lax.axis_index(bit[0]) >> bit[1]) & 1


def pick(values, index, axis):
    return lax.dynamic_index_in_dim(values, index, axis, keepdims=False)


def column_groups(total, groups):
    unit = total // groups // 128 * 128
    edges = [unit * at for at in range(groups)] + [total]
    return list(zip(edges[:-1], edges[1:]))


def reduce_rows(left, right, groups):
    emb_bits, seq_bits = axis_bits("emb"), axis_bits("seq")
    names = emb_bits[::-1] + seq_bits[::-1]
    rows = left.shape[1]
    first = names[len(emb_bits) - 1]
    others = emb_bits[1:2] + seq_bits[:2]
    tail = emb_bits[2:] + seq_bits[2:]
    at = names.index(first)
    piece = rows >> (at + 1)
    mine_bit = own_bit(first)

    def half(which):
        cuts = [
            lax.dynamic_slice_in_dim(left, (2 * part + which) * piece, piece, 1)
            for part in range(1 << at)
        ]
        return jnp.concatenate(cuts, axis=1)

    halves = {"kept": half(mine_bit), "sent": half(1 - mine_bit)}

    def product(which, low, high):
        return jnp.dot(
            halves[which].T, right[:, low:high], preferred_element_type=jnp.float32
        )

    spans = column_groups(right.shape[1], groups)
    live = []
    arrived = [swap_with(product("sent", *span).astype(jnp.bfloat16), first) for span in spans]
    for span, part in zip(spans, arrived):
        total = (product("kept", *span) + part.astype(jnp.float32)).astype(jnp.bfloat16)
        live.append(total)
    left_names = [name for name in names if name != first]
    state = []
    for at_group, total in enumerate(live):
        turn = at_group % len(others)
        order = others[turn:] + others[:turn] + tail
        state.append([total, list(left_names), order])
    for step in range(len(left_names)):
        for entry in state:
            total, held, order = entry
            bit = order[step]
            place = held.index(bit)
            width = total.shape[-1]
            shaped = total.reshape(1 << place, 2, total.shape[0] >> (place + 1), width)
            mine_bit = own_bit(bit)
            sent = pick(shaped, 1 - mine_bit, 1)
            kept = pick(shaped, mine_bit, 1)
            arrived = swap_with(sent, bit)
            summed = kept.astype(jnp.float32) + arrived.astype(jnp.float32)
            if step + 1 < len(left_names):
                summed = summed.astype(jnp.bfloat16)
            entry[0] = summed.reshape(total.shape[0] // 2, width)
            held.remove(bit)
    return jnp.concatenate([entry[0] for entry in state], axis=1)


def shards(
    item_ids, action_ids, hist_len, hist_owner, item_table, action_table, w_in, w_out, cotangent
):
    emb_count = lax.axis_size("emb")
    seq_count = lax.axis_size("seq")
    device_count = emb_count * seq_count
    owner_count = item_ids.shape[0]
    slot_rows = item_ids.shape[1]
    column_width = item_table.shape[1]
    looked_items = jnp.take(item_table, item_ids, axis=0).astype(jnp.float32)
    action_hot = (
        action_ids[:, :, None] == jnp.arange(action_table.shape[0], dtype=jnp.int32)
    ).astype(jnp.bfloat16)
    looked_actions = jnp.einsum(
        "osa,ac->osc", action_hot, action_table, preferred_element_type=jnp.float32
    )
    looked = (looked_items + looked_actions).astype(jnp.bfloat16)
    arrived = lax.all_to_all(looked, ("emb", "seq"), split_axis=0, concat_axis=0, tiled=True)
    x_rows = (
        arrived.reshape(emb_count, seq_count, slot_rows, column_width)
        .transpose(1, 2, 0, 3)
        .reshape(seq_count * slot_rows, emb_count * column_width)
    )
    owner_index = lax.axis_index(("emb", "seq"))
    slot_start, occupied = slot_layout(hist_len, hist_owner, owner_index, x_rows.shape[0])
    x_rows = x_rows * occupied[:, None]
    gated_grad = jnp.dot(cotangent, w_out.T, preferred_element_type=jnp.float32).astype(
        jnp.bfloat16
    )
    result, input_grad, normed, pre_grad, out_share = local_pass(
        x_rows, cotangent, slot_start, occupied, w_in, w_out, gated_grad
    )
    outgoing = (
        input_grad.reshape(seq_count, slot_rows, emb_count, column_width)
        .transpose(2, 0, 1, 3)
        .reshape(owner_count, slot_rows, column_width)
    )
    row_grads = lax.all_to_all(outgoing, ("emb", "seq"), split_axis=0, concat_axis=0, tiled=True)
    in_share = reduce_rows(normed, pre_grad, 3)
    return (result, row_grads, in_share / device_count, out_share / device_count)


def solution(mesh):
    in_specs = (
        P(None, "seq"),
        P(None, "seq"),
        P(),
        P(),
        P(None, "emb"),
        P(None, "emb"),
        P(),
        P(),
        P(("emb", "seq"), None),
    )
    out_specs = (
        P(("emb", "seq"), None),
        P(None, "seq", "emb"),
        P(("emb", "seq"), None),
        P(("emb", "seq"), None),
    )

    return jax.shard_map(shards, mesh=mesh, in_specs=in_specs, out_specs=out_specs, check_vma=False)
```

```python
import jax
import jax.numpy as jnp
from jax import lax
from jax.experimental import pallas as pl
from jax.experimental.pallas import tpu as pltpu
from jax.sharding import PartitionSpec as P

D = 1024
HEADS = 4
HEAD = 256
CAP = 512
TILE = 256
GROUPS = 3
STRIP = 16
NT = (((1,), (1,)), ((), ()))
TN = (((0,), (0,)), ((), ()))


EPSILON = 1e-06


def layer_norm(values):
    centred = values - jnp.mean(values, axis=-1, keepdims=True)
    spread = jnp.mean(centred * centred, axis=-1, keepdims=True)
    return centred * lax.rsqrt(spread + EPSILON)


def slot_layout(hist_len, hist_owner, owner_index, slot_count):
    chosen = hist_owner == owner_index
    lengths = jnp.where(chosen, hist_len, 0)
    hist_ends = jnp.cumsum(lengths, dtype=jnp.int32)
    starts = hist_ends - lengths
    slot_index = jnp.arange(slot_count, dtype=jnp.int32)
    inside = (
        chosen[None, :]
        & (starts[None, :] <= slot_index[:, None])
        & (slot_index[:, None] < hist_ends[None, :])
    )
    slot_start = jnp.sum(jnp.where(inside, starts[None, :], 0), axis=1, dtype=jnp.int32)
    occupied = jnp.any(inside, axis=1)
    return (slot_start, occupied)


def head_weights(queries, keys, lower_ref, row_at, limit):
    tile = queries.shape[0]
    scaled = (
        lax.dot_general(queries, keys, NT, preferred_element_type=jnp.float32) * HEAD ** (-0.5)
    )
    rows = row_at + lax.broadcasted_iota(jnp.int32, (tile, limit), 0)
    columns = lax.broadcasted_iota(jnp.int32, (tile, limit), 1)
    allowed = (columns <= rows) & (columns >= lower_ref[pl.ds(row_at, tile), :])
    return scaled, jax.nn.sigmoid(scaled), allowed


def mixing_kernel(lower_ref, gate_ref, value_ref, query_ref, key_ref, mixed_ref, gated_ref, held):
    head = pl.program_id(0)
    row_count = value_ref.shape[0]
    held[0] = jax.nn.silu(value_ref[...]).astype(jnp.bfloat16)
    held[1] = jax.nn.silu(query_ref[...]).astype(jnp.bfloat16)
    held[2] = jax.nn.silu(key_ref[...]).astype(jnp.bfloat16)
    columns = pl.ds(pl.multiple_of(head * HEAD, HEAD), HEAD)
    for row_at in range(0, row_count, TILE):
        limit = row_at + TILE
        scaled, sigmoid, allowed = head_weights(
            held[1, row_at:limit, :], held[2, :limit, :], lower_ref, row_at, limit
        )
        weights = jnp.where(allowed, scaled * sigmoid / CAP, 0.0).astype(jnp.bfloat16)
        mixed_ref[row_at:limit, columns] = jnp.dot(
            weights, held[0, :limit, :], preferred_element_type=jnp.float32
        )

    @pl.when(head == HEADS - 1)
    def finish():
        def rows_step(at, carry):
            rows = pl.ds(pl.multiple_of(at * STRIP, STRIP), STRIP)
            gate = jax.nn.silu(gate_ref[rows, :]).astype(jnp.bfloat16).astype(jnp.float32)
            gated_ref[rows, :] = (layer_norm(mixed_ref[rows, :]) * gate).astype(jnp.bfloat16)
            return carry

        lax.fori_loop(0, row_count // STRIP, rows_step, 0)


def silu_back(pre_values, grads):
    sigmoid = jax.nn.sigmoid(pre_values)
    rounded = grads.astype(jnp.bfloat16).astype(jnp.float32)
    return (rounded * (sigmoid * (1.0 + pre_values * (1.0 - sigmoid)))).astype(jnp.bfloat16)


def mixing_back_kernel(
    lower_ref,
    gate_ref,
    value_ref,
    query_ref,
    key_ref,
    mixed_ref,
    grad_ref,
    out_ref,
    mixed_grad,
    held,
    value_sum,
    key_sum,
):
    head = pl.program_id(0)
    row_count = value_ref.shape[0]

    @pl.when(head == 0)
    def begin():
        def rows_step(at, carry):
            rows = pl.ds(pl.multiple_of(at * STRIP, STRIP), STRIP)
            pre_gate = gate_ref[rows, :]
            gate = jax.nn.silu(pre_gate).astype(jnp.bfloat16).astype(jnp.float32)
            grads = grad_ref[rows, :].astype(jnp.float32)
            values = mixed_ref[rows, :]
            centred = values - jnp.mean(values, axis=-1, keepdims=True)
            inverse = lax.rsqrt(jnp.mean(centred * centred, axis=-1, keepdims=True) + EPSILON)
            normal = centred * inverse
            out_ref[rows, :D] = silu_back(pre_gate, grads * normal)
            back = grads * gate
            along = jnp.mean(back * normal, axis=-1, keepdims=True)
            level = jnp.mean(back, axis=-1, keepdims=True)
            mixed_grad[rows, :] = (inverse * (back - level - normal * along)).astype(jnp.bfloat16)
            return carry

        lax.fori_loop(0, row_count // STRIP, rows_step, 0)

    held[0] = jax.nn.silu(value_ref[...]).astype(jnp.bfloat16)
    held[1] = jax.nn.silu(query_ref[...]).astype(jnp.bfloat16)
    held[2] = jax.nn.silu(key_ref[...]).astype(jnp.bfloat16)
    columns = pl.ds(pl.multiple_of(head * HEAD, HEAD), HEAD)
    value_sum[...] = jnp.zeros_like(value_sum)
    key_sum[...] = jnp.zeros_like(key_sum)
    for row_at in range(0, row_count, TILE):
        limit = row_at + TILE
        queries, keys = held[1, row_at:limit, :], held[2, :limit, :]
        scaled, sigmoid, allowed = head_weights(queries, keys, lower_ref, row_at, limit)
        weights = jnp.where(allowed, scaled * sigmoid / CAP, 0.0).astype(jnp.bfloat16)
        rows_grad = mixed_grad[row_at:limit, columns]
        value_sum[:limit, :] += lax.dot_general(
            weights, rows_grad, TN, preferred_element_type=jnp.float32
        )
        weight_grad = lax.dot_general(
            rows_grad, held[0, :limit, :], NT, preferred_element_type=jnp.float32
        ).astype(jnp.bfloat16).astype(jnp.float32)
        score_grad = jnp.where(
            allowed,
            weight_grad * (sigmoid * (1.0 + scaled * (1.0 - sigmoid))) * (HEAD ** (-0.5) / CAP),
            0.0,
        ).astype(jnp.bfloat16)
        query_grad = jnp.dot(score_grad, keys, preferred_element_type=jnp.float32)
        place = pl.ds(pl.multiple_of(2 * D + head * HEAD, HEAD), HEAD)
        out_ref[row_at:limit, place] = silu_back(query_ref[row_at:limit, :], query_grad)
        key_sum[:limit, :] += lax.dot_general(
            score_grad, queries, TN, preferred_element_type=jnp.float32
        )
    place = pl.ds(pl.multiple_of(D + head * HEAD, HEAD), HEAD)
    out_ref[:, place] = silu_back(value_ref[...], value_sum[...])
    place = pl.ds(pl.multiple_of(3 * D + head * HEAD, HEAD), HEAD)
    out_ref[:, place] = silu_back(key_ref[...], key_sum[...])


def part_specs(rows):
    return [
        pl.BlockSpec((rows, 1), lambda head: (0, 0)),
        pl.BlockSpec((rows, D), lambda head: (0, 0)),
        pl.BlockSpec((rows, HEAD), lambda head: (0, HEADS + head)),
        pl.BlockSpec((rows, HEAD), lambda head: (0, 2 * HEADS + head)),
        pl.BlockSpec((rows, HEAD), lambda head: (0, 3 * HEADS + head)),
    ]


def mix(lower, pre_act):
    rows = pre_act.shape[0]
    whole = pl.BlockSpec((rows, D), lambda head: (0, 0))
    return pl.pallas_call(
        mixing_kernel,
        grid=(HEADS,),
        in_specs=part_specs(rows),
        out_specs=[whole, whole],
        out_shape=[
            jax.ShapeDtypeStruct((rows, D), jnp.float32),
            jax.ShapeDtypeStruct((rows, D), jnp.bfloat16),
        ],
        scratch_shapes=[pltpu.VMEM((3, rows, HEAD), jnp.bfloat16)],
        compiler_params=pltpu.CompilerParams(vmem_limit_bytes=40 * 2**20),
        cost_estimate=pl.CostEstimate(flops=10**10, bytes_accessed=14 * 2**20, transcendentals=0),
    )(lower, pre_act, pre_act, pre_act, pre_act)


def mix_back(lower, pre_act, mixed, gated_grad):
    rows = pre_act.shape[0]
    whole = pl.BlockSpec((rows, D), lambda head: (0, 0))
    return pl.pallas_call(
        mixing_back_kernel,
        grid=(HEADS,),
        in_specs=part_specs(rows) + [whole, whole],
        out_specs=pl.BlockSpec((rows, 4 * D), lambda head: (0, 0)),
        out_shape=jax.ShapeDtypeStruct((rows, 4 * D), jnp.bfloat16),
        scratch_shapes=[
            pltpu.VMEM((rows, D), jnp.bfloat16),
            pltpu.VMEM((3, rows, HEAD), jnp.bfloat16),
            pltpu.VMEM((rows, HEAD), jnp.float32),
            pltpu.VMEM((rows, HEAD), jnp.float32),
        ],
        compiler_params=pltpu.CompilerParams(vmem_limit_bytes=48 * 2**20),
        cost_estimate=pl.CostEstimate(
            flops=2 * 10**10, bytes_accessed=18 * 2**20, transcendentals=0
        ),
    )(lower, pre_act, pre_act, pre_act, pre_act, mixed, gated_grad)


def local_pass(x_rows, grad_rows, slot_start, occupied, w_in, w_out, gated_grad):
    row_count = x_rows.shape[0]
    normed = layer_norm(x_rows.astype(jnp.float32)).astype(jnp.bfloat16)
    pre_act = jnp.dot(normed, w_in, preferred_element_type=jnp.float32)
    lower = jnp.where(occupied, slot_start, row_count)[:, None]
    mixed, gated_rows = mix(lower, pre_act)
    result = (
        x_rows.astype(jnp.float32) + jnp.dot(gated_rows, w_out, preferred_element_type=jnp.float32)
    ).astype(jnp.bfloat16)
    pre_grad = mix_back(lower, pre_act, mixed, gated_grad)
    rights = (pre_grad, grad_rows)
    spans = core_spans([right.shape[1] for right in rights], GROUPS)
    in_sent, in_kept = core_halves(normed)
    out_sent, out_kept = core_halves(gated_rows)
    sent = [
        partial((in_sent, out_sent)[source], rights[source], low, high).astype(jnp.bfloat16)
        for group, source, low, high in spans
    ]
    held_grad, sent = lax.optimization_barrier((pre_grad, sent))
    shares = reduce_rows(spans, sent, (in_kept, out_kept), rights, GROUPS)
    normed_grad = jnp.dot(held_grad, w_in.T, preferred_element_type=jnp.float32).astype(jnp.bfloat16)
    unused_value, norm_back = jax.vjp(layer_norm, x_rows.astype(jnp.float32))
    input_grad = (
        norm_back(normed_grad.astype(jnp.float32))[0] + grad_rows.astype(jnp.float32)
    ) * occupied[:, None]
    return (result, input_grad.astype(jnp.bfloat16), *shares)


def axis_bits(name):
    return [(name, bit) for bit in range(lax.axis_size(name).bit_length() - 1)]


def swap_with(values, bit):
    name, place = bit
    count = lax.axis_size(name)
    return lax.ppermute(values, name, [(at, at ^ (1 << place)) for at in range(count)])


def own_bit(bit):
    return (lax.axis_index(bit[0]) >> bit[1]) & 1


def pick(values, index, axis):
    return lax.dynamic_index_in_dim(values, index, axis, keepdims=False)


def column_edges(widths, groups):
    unit = sum(widths) // groups // 128 * 128
    return [unit * at for at in range(groups)] + [sum(widths)]


def first_layout():
    names = axis_bits("emb")[::-1] + axis_bits("seq")[::-1]
    first = ("emb", 0)
    return names, first, names.index(first)


def core_halves(left):
    names, first, at = first_layout()
    piece = left.shape[1] >> (at + 1)

    def half(which):
        cuts = [
            lax.dynamic_slice_in_dim(left, (2 * part + which) * piece, piece, 1)
            for part in range(1 << at)
        ]
        return jnp.concatenate(cuts, axis=1).T

    return half(1 - own_bit(first)), half(own_bit(first))


def core_spans(widths, groups):
    edges = column_edges(widths, groups)
    spans, start = [], 0
    for source, width in enumerate(widths):
        for group in range(groups):
            low, high = max(edges[group], start), min(edges[group + 1], start + width)
            if low < high:
                spans.append((group, source, low - start, high - start))
        start += width
    return spans


def partial(left, right, low, high):
    return jnp.dot(left, right[:, low:high], preferred_element_type=jnp.float32)


def reduce_rows(spans, sent, kept, rights, groups):
    names, first, _ = first_layout()
    emb_bits, seq_bits = axis_bits("emb"), axis_bits("seq")
    others = emb_bits[1:2] + seq_bits[:2]
    tail = emb_bits[2:] + seq_bits[2:]
    arrived = [swap_with(part, first) for part in sent]
    live = [[] for _ in range(groups)]
    for (group, source, low, high), part in zip(spans, arrived):
        total = partial(kept[source], rights[source], low, high) + part.astype(jnp.float32)
        live[group].append(total.astype(jnp.bfloat16))
    state = []
    for group, parts in enumerate(live):
        turn = group % len(others)
        order = others[turn:] + others[:turn] + tail
        total = parts[0] if len(parts) == 1 else jnp.concatenate(parts, axis=1)
        state.append([total, [name for name in names if name != first], order])
    for step in range(len(names) - 1):
        for entry in state:
            total, held, order = entry
            bit = order[step]
            place = held.index(bit)
            width = total.shape[-1]
            shaped = total.reshape(1 << place, 2, total.shape[0] >> (place + 1), width)
            mine_bit = own_bit(bit)
            outgoing = pick(shaped, 1 - mine_bit, 1)
            staying = pick(shaped, mine_bit, 1)
            summed = staying.astype(jnp.float32) + swap_with(outgoing, bit).astype(jnp.float32)
            if step + 2 < len(names):
                summed = summed.astype(jnp.bfloat16)
            entry[0] = summed.reshape(total.shape[0] // 2, width)
            held.remove(bit)
    joined = jnp.concatenate([entry[0] for entry in state], axis=1)
    cut = rights[0].shape[1]
    return joined[:, :cut], joined[:, cut:]


def shards(
    item_ids, action_ids, hist_len, hist_owner, item_table, action_table, w_in, w_out, cotangent
):
    emb_count = lax.axis_size("emb")
    seq_count = lax.axis_size("seq")
    device_count = emb_count * seq_count
    owner_count = item_ids.shape[0]
    slot_rows = item_ids.shape[1]
    column_width = item_table.shape[1]
    looked_items = jnp.take(item_table, item_ids, axis=0).astype(jnp.float32)
    action_hot = (
        action_ids[:, :, None] == jnp.arange(action_table.shape[0], dtype=jnp.int32)
    ).astype(jnp.bfloat16)
    looked_actions = jnp.einsum(
        "osa,ac->osc", action_hot, action_table, preferred_element_type=jnp.float32
    )
    looked = (looked_items + looked_actions).astype(jnp.bfloat16)
    arrived = lax.all_to_all(looked, ("emb", "seq"), split_axis=0, concat_axis=0, tiled=True)
    x_rows = (
        arrived.reshape(emb_count, seq_count, slot_rows, column_width)
        .transpose(1, 2, 0, 3)
        .reshape(seq_count * slot_rows, emb_count * column_width)
    )
    owner_index = lax.axis_index(("emb", "seq"))
    slot_start, occupied = slot_layout(hist_len, hist_owner, owner_index, x_rows.shape[0])
    x_rows = x_rows * occupied[:, None]
    gated_grad = jnp.dot(cotangent, w_out.T, preferred_element_type=jnp.float32).astype(
        jnp.bfloat16
    )
    result, input_grad, in_share, out_share = local_pass(
        x_rows, cotangent, slot_start, occupied, w_in, w_out, gated_grad
    )
    outgoing = (
        input_grad.reshape(seq_count, slot_rows, emb_count, column_width)
        .transpose(2, 0, 1, 3)
        .reshape(owner_count, slot_rows, column_width)
    )
    row_grads = lax.all_to_all(outgoing, ("emb", "seq"), split_axis=0, concat_axis=0, tiled=True)
    return (result, row_grads, in_share / device_count, out_share / device_count)


def solution(mesh):
    in_specs = (
        P(None, "seq"),
        P(None, "seq"),
        P(),
        P(),
        P(None, "emb"),
        P(None, "emb"),
        P(),
        P(),
        P(("emb", "seq"), None),
    )
    out_specs = (
        P(("emb", "seq"), None),
        P(None, "seq", "emb"),
        P(("emb", "seq"), None),
        P(("emb", "seq"), None),
    )
    return jax.shard_map(shards, mesh=mesh, in_specs=in_specs, out_specs=out_specs, check_vma=False)
```
